256 devices in a mesh: dp: 32 (over y, z), mp: 8 (over x, core).
Axes of the slice: x: 4, y: 4, z: 8, core: 2. Of those that a mesh axis runs over, the one named last changes fastest.
Arguments:
- inputs: bfloat16 [12288, 4608], P('dp', 'mp'), may hold values from -80 to 80
- queries: bfloat16 [12288, 4096], P('dp', 'mp'), may hold values from -7.5 to 7.5
- keys: bfloat16 [12288, 2048], P('dp', 'mp'), may hold values from -7.5 to 7.5
- values: bfloat16 [12288, 2048], P('dp', 'mp'), may hold values from -6 to 6
- out_weight: bfloat16 [4096, 4608], P('mp'), may hold values from -0.5 to 0.5
- norm_gain: bfloat16 [4608], P('mp'), may hold values from 0.5 to 1.5
- languages: int32 [32, 1], replicated, may hold values from 0 to 7
- lengths: int32 [32], replicated, may hold values from 193 to 384, as said below
- pattern: int32 [32, 3, 3], P('dp'), may hold values from 0 to 1, as said below
Outputs:
- counts: int32 [8], replicated
- mean: float32 [8, 4608], P(None, 'dp')
- co_moment: float32 [8, 4608, 4608], P(None, 'dp', 'mp')
The draws below stay inside these ranges and needn't reach their ends.
Inputs may be any that keep to these rules, and one draw needn't show every extreme that they name: Each of the 8 languages is the language of one or more sequences. `lengths`: one or more sequences have all 384 tokens live. `pattern`: for each sequence there is a window w of 1 to 3 blocks such that block (q, k) is 1 exactly when q - w < k <= q.
All inputs are finite; a program needn't handle non-finite values.
Results may differ from the reference program's by a relative error of at most 0.01.
Values may be sent and summed in bfloat16 or wider, within the bound.
No kernel may reach another device: no remote copies, remote signals or barrier semaphores. Data moves between devices by JAX's collectives and lax.ppermute only.
A program may use at most 128 MiB of HBM per device.

```python
import math
import jax
import jax.numpy as jnp
from jax import lax

D = 4608
H = 32
KVH = 16
HD = 128
SEQ_LEN = 384
LANGS = 8
BLK = 128
NB = 3
SEQS = 32
TOKENS = 12288


def draw_inputs(key, part):
    base = jnp.clip(jax.random.normal(key, (TOKENS, D), jnp.float32), -5.0, 5.0)
    ramp = jnp.arange(D, dtype=jnp.float32) / D
    jitter = jax.random.uniform(jax.random.fold_in(key, 1), (D,), jnp.float32)
    column = 0.25 * jnp.exp(math.log(10.0) * (ramp + 0.3 * jitter))
    return (base * column[None, :]).astype(jnp.bfloat16)


def alignment(key):
    direction = 2.0 * jax.random.randint(jax.random.fold_in(key, 11), (HD,), 0, 2).astype(jnp.float32) - 1.0
    quarter = jax.random.randint(jax.random.fold_in(key, 12), (SEQS,), 0, 4)
    forced = jax.random.randint(jax.random.fold_in(key, 13), (), 0, SEQS)
    chosen = (quarter < 2) | (jnp.arange(SEQS) == forced)
    token_pick = jax.random.randint(jax.random.fold_in(key, 14), (SEQS, SEQ_LEN), 0, 2)
    active = (chosen[:, None] & (token_pick == 1)).reshape(TOKENS).astype(jnp.float32)
    return (direction, active)


def drawn_heads(key, salt, heads):
    direction, active = alignment(key)
    base = jnp.clip(jax.random.normal(jax.random.fold_in(key, salt), (TOKENS, heads, HD), jnp.float32), -4.0, 4.0)
    amplitude = jax.random.uniform(jax.random.fold_in(key, salt + 1), (TOKENS,), jnp.float32, 1.8, 3.2)
    shifted = base + (active * amplitude)[:, None, None] * direction[None, None, :]
    return jnp.clip(shifted, -7.5, 7.5).reshape(TOKENS, heads * HD)


def draw_queries(key, part):
    return drawn_heads(key, 31, H).astype(jnp.bfloat16)


def draw_keys(key, part):
    return drawn_heads(key, 41, KVH).astype(jnp.bfloat16)


def draw_lengths(key, part):
    dropped = jax.random.randint(key, (SEQS,), 0, SEQ_LEN // 2)
    chosen = jax.random.randint(jax.random.fold_in(key, 1), (), 0, SEQS)
    return jnp.where(jnp.arange(SEQS) == chosen, SEQ_LEN, SEQ_LEN - dropped).astype(jnp.int32)


def draw_pattern(key, part):
    window = jax.random.randint(key, (SEQS, 1, 1), 1, NB + 1)
    query_block = jnp.arange(NB)[None, :, None]
    key_block = jnp.arange(NB)[None, None, :]
    return ((key_block <= query_block) & (key_block > query_block - window)).astype(jnp.int32)


def levels(own_key, dims, split, low, high):
    level = 1.0
    for dim, blocks in split:
        draws = jax.random.uniform(jax.random.fold_in(jax.random.fold_in(own_key, 6), dim), (blocks,), jnp.float32, low / len(split), high / len(split))
        level = level * jnp.repeat(jnp.exp(draws), dims[dim] // blocks).reshape((-1,) + (1,) * (len(dims) - 1 - dim))
    return level


def choose_distinct(key, rows, count, top, lift):
    sequence = jax.random.permutation(jax.random.fold_in(key, 1), count)
    favour = sequence
    for power in range(3):
        favour = favour * favour // count
    favour = favour * lift // count
    lots = jax.random.randint(jax.random.fold_in(key, 2), (rows, count), 0, 4096) + favour
    sure = jax.random.permutation(jax.random.fold_in(key, 3), rows)[jnp.arange(count) % rows]
    lots = jnp.where(jnp.arange(rows)[:, None] == sure[None, :], 1 << 14, lots)
    score = lots * count + jnp.arange(count)
    return lax.top_k(score.astype(jnp.int32), top)[1].astype(jnp.int32)


def bell_draw(stream_key, shape, deviation, bound, cuts=(), kind=jnp.bfloat16):
    values = jax.random.normal(stream_key, shape, jnp.float32) * deviation
    if len(cuts) > 0:
        values = levels(stream_key, shape, cuts, -0.22, 0.18) * values
    return jnp.clip(values, min=-bound, max=bound).astype(kind)


def setup_inputs(seed: int = 0) -> dict:
    streams_of = jax.random.split(jax.random.key(seed), 10)
    inputs = draw_inputs(jax.random.fold_in(streams_of[9], 71), 0)
    queries = draw_queries(jax.random.fold_in(streams_of[9], 71), 0)
    keys = draw_keys(jax.random.fold_in(streams_of[9], 71), 0)
    values = bell_draw(streams_of[3], (TOKENS, KVH * HD), 1.0, 6.0, ((0, 32), (1, 8)))
    out_weight = bell_draw(streams_of[4], (H * HD, D), HD ** -0.5, 0.5, ((0, 8),))
    norm_gain = jnp.clip(1.0 + 0.1 * jax.random.normal(streams_of[5], (D,), jnp.float32), 0.5, 1.5).astype(jnp.bfloat16)
    languages = choose_distinct(streams_of[6], SEQS, LANGS, 1, 2048)
    lengths = draw_lengths(jax.random.fold_in(streams_of[9], 71), 0)
    pattern = draw_pattern(jax.random.fold_in(streams_of[9], 71), 0)
    return {"inputs": inputs, "queries": queries, "keys": keys, "values": values, "out_weight": out_weight, "norm_gain": norm_gain, "languages": languages, "lengths": lengths, "pattern": pattern}


query_scale = 1.0 / 12.0
softcap = 50.0
epsilon = 1e-06

def visible(blocks, seq_len):
    spread = jnp.repeat(jnp.repeat(blocks, BLK, 0), BLK, 1)
    position = jnp.arange(seq_len)
    return (spread == 1) & (position[None, :] <= position[:, None])

def attend(queries_seq, keys_seq, values_seq, blocks):
    seq_len = queries_seq.shape[0]
    grouped = queries_seq.reshape(seq_len, KVH, H // KVH, HD).astype(jnp.float32)
    keyed = keys_seq.reshape(seq_len, KVH, HD).astype(jnp.float32)
    valued = values_seq.reshape(seq_len, KVH, HD).astype(jnp.float32)
    scores = jnp.einsum('qkgd,tkd->kgqt', grouped, keyed) * query_scale
    capped = softcap * jnp.tanh(scores / softcap)
    allowed = visible(blocks, seq_len)
    expo = jnp.where(allowed, jnp.exp(capped), 0.0)
    weights = (expo / lax.optimization_barrier(jnp.sum(expo, -1, keepdims=True))).astype(jnp.bfloat16)
    mixed = jnp.einsum('kgqt,tkd->qkgd', weights.astype(jnp.float32), valued)
    return mixed.astype(jnp.bfloat16).reshape(seq_len, H * HD)

def reference(inputs, queries, keys, values, out_weight, norm_gain, languages, lengths, pattern):
    query_seqs = queries.reshape(SEQS, SEQ_LEN, H * HD)
    key_seqs = keys.reshape(SEQS, SEQ_LEN, KVH * HD)
    value_seqs = values.reshape(SEQS, SEQ_LEN, KVH * HD)
    mixed = lax.map(lambda item: attend(item[0], item[1], item[2], item[3]), (query_seqs, key_seqs, value_seqs, pattern)).reshape(TOKENS, H * HD)
    output = jnp.dot(mixed, out_weight, preferred_element_type=jnp.float32)
    hidden = inputs.astype(jnp.float32) + output
    square = lax.optimization_barrier(jnp.sum(hidden * hidden, -1, keepdims=True))
    normed = (hidden * lax.rsqrt(square / D + epsilon) * norm_gain.astype(jnp.float32)[None, :]).astype(jnp.bfloat16)
    normed_seqs = normed.reshape(SEQS, SEQ_LEN, D)
    language = languages[:, 0]
    live = jnp.arange(SEQ_LEN)[None, :] < lengths[:, None]

    def absorb(carry, item):
        products, sums = carry
        rows, alive, which = item
        masked = rows * alive.astype(jnp.bfloat16)[:, None]
        term = jnp.dot(masked.T, rows, preferred_element_type=jnp.float32)
        products = lax.dynamic_update_index_in_dim(products, lax.dynamic_index_in_dim(products, which, 0, False) + term, which, 0)
        row_total = lax.optimization_barrier(jnp.sum(masked.astype(jnp.float32), 0))
        sums = lax.dynamic_update_index_in_dim(sums, lax.dynamic_index_in_dim(sums, which, 0, False) + row_total, which, 0)
        return ((products, sums), None)
    start_state = (jnp.zeros((LANGS, D, D), jnp.float32), jnp.zeros((LANGS, D), jnp.float32))
    (products, sums), _ = lax.scan(absorb, start_state, (normed_seqs, live, language))
    onehot = (language[:, None] == jnp.arange(LANGS)[None, :]).astype(jnp.int32)
    counts = lax.optimization_barrier(jnp.sum(onehot * lengths[:, None], 0))
    scale = counts.astype(jnp.float32)
    mean = sums / scale[:, None]
    co_moment = (products - sums[:, :, None] * sums[:, None, :] / scale[:, None, None]) / scale[:, None, None]
    return (counts, mean, co_moment)
```

```python
import functools
import jax
import jax.numpy as jnp
from jax import lax
from jax.experimental import pallas as pl
from jax.experimental.pallas import tpu as pltpu
from jax.sharding import PartitionSpec as P

D = 4608
H = 32
KVH = 16
HD = 128
SEQ = 384
SEQS = 32
LANGS = 8
BLK = 128
NY, NZ, NX = 4, 8, 4
PANEL = 576
ROW = 144
LROW = 160

query_scale = 1.0 / 12.0
softcap = 50.0
epsilon = 1e-06


F32 = jnp.float32
BF16 = jnp.bfloat16
NT = (((1,), (1,)), ((), ()))


def visible(blocks, seq_len):
    spread = jnp.repeat(jnp.repeat(blocks, BLK, 0), BLK, 1)
    position = jnp.arange(seq_len)
    return (spread == 1) & (position[None, :] <= position[:, None])


def attend(queries, keys, values, blocks):
    seq_len = queries.shape[0]
    kv_local = keys.shape[1] // HD
    grouped = queries.reshape(seq_len, kv_local, H // KVH, HD)
    keyed = keys.reshape(seq_len, kv_local, HD)
    valued = values.reshape(seq_len, kv_local, HD)
    scores = (
        jnp.einsum("qkgd,tkd->kgqt", grouped, keyed, preferred_element_type=jnp.float32)
        * query_scale
    )
    capped = softcap * jnp.tanh(scores / softcap)
    allowed = visible(blocks, seq_len)
    expo = jnp.where(allowed, jnp.exp(capped), 0.0)
    weights = (expo / jnp.sum(expo, -1, keepdims=True)).astype(jnp.bfloat16)
    mixed = jnp.einsum("kgqt,tkd->qkgd", weights, valued, preferred_element_type=jnp.float32)
    return mixed.astype(jnp.bfloat16).reshape(seq_len, kv_local * (H // KVH) * HD)


def dp_id(y, z):
    return (y % NY) * NZ + z % NZ


def mp_id(x, c):
    return (x % NX) * 2 + c


def dp_step(block, sy, sz):
    return lax.ppermute(
        block, "dp", [(dp_id(y, z), dp_id(y + sy, z + sz)) for y in range(NY) for z in range(NZ)]
    )


def x_step(block, s):
    return lax.ppermute(
        block, "mp", [(mp_id(x, c), mp_id(x + s, c)) for x in range(NX) for c in range(2)]
    )


def core_swap(block):
    return lax.ppermute(
        block, "mp", [(mp_id(x, c), mp_id(x, 1 - c)) for x in range(NX) for c in range(2)]
    )


TREE = [
    ((0, 1), 0, 1), ((0, -1), 0, -1), ((1, 0), 1, 0), ((-1, 0), -1, 0),
    ((0, 2), 0, 1), ((0, -2), 0, -1), ((1, 1), 1, 0), ((-1, -1), -1, 0),
    ((0, 3), 0, 1), ((0, -3), 0, -1), ((1, -1), 1, 0), ((-1, 1), -1, 0),
    ((1, 2), 0, 1), ((-1, -2), 0, -1), ((2, 1), 1, 0), ((-1, -3), -1, 0),
    ((-1, 2), 0, 1), ((1, -2), 0, -1), ((1, 3), 1, 0), ((2, -1), -1, 0),
    ((2, 2), 0, 1), ((-1, 4), 0, -1), ((1, -3), 1, 0), ((2, -3), -1, 0),
    ((1, 4), 0, 1), ((2, -2), 0, -1), ((2, 3), 1, 0), ((-1, 3), -1, 0),
    ((0, 4), 0, 1), ((2, 4), 0, -1), ((2, 0), -1, 0),
]
GROUPS = (8, 8, 8, 4, 4)


def canon(dy, dz):
    return (dy % NY, dz % NZ)


def gather_all(block):
    have = {(0, 0): block}
    order = [(0, 0)]
    for n, ((dy, dz), sy, sz) in enumerate(TREE):
        key = canon(dy, dz)
        with jax.named_scope(f"tree{n}"):
            have[key] = dp_step(have[canon(dy - sy, dz - sz)], sy, sz)
        order.append(key)
    return order, [have[k] for k in order]


def gram_kernel(first, size, last, meta, count, gain, left, *rest):
    rights = rest[:size]
    rest = rest[size:]
    if not first:
        acc_in, row_in, col_in = rest[:3]
        rest = rest[3:]
    if last:
        mean_out, co_out, acc, row_acc, col_acc = rest[:5]
        rest = rest[5:]
    else:
        acc, row_acc, col_acc = rest[:3]
        rest = rest[3:]
    right_buf, left_buf, right_sem, left_sem = rest
    for i in range(size):
        pltpu.make_async_copy(rights[i], right_buf.at[i], right_sem.at[i]).start()
        pltpu.make_async_copy(left.at[meta[2, i], meta[3, i]], left_buf.at[i], left_sem.at[i]).start()
    if first:
        acc[...] = jnp.zeros_like(acc)
        row_acc[...] = jnp.zeros_like(row_acc)
        col_acc[...] = jnp.zeros_like(col_acc)
    elif last:
        acc[...] = acc_in[...]
        row_acc[...] = row_in[...]
        col_acc[...] = col_in[...]
    token = lax.broadcasted_iota(jnp.int32, (1, SEQ), 1)
    ones = jnp.ones((BLK, SEQ), BF16)

    def step(i, carry):
        pltpu.make_async_copy(rights[0], right_buf.at[i], right_sem.at[i]).wait()
        pltpu.make_async_copy(left.at[0, 0], left_buf.at[i], left_sem.at[i]).wait()
        which = meta[0, i]
        live = (token < meta[1, i]).astype(F32)
        part = left_buf[i]
        scale = part[ROW : ROW + 1].astype(F32) + part[ROW + 1 : ROW + 2].astype(F32)
        rows = part[:ROW].astype(F32) * live
        extra = part[ROW:].astype(F32) * live
        lhs = jnp.concatenate([(rows * scale).astype(BF16), extra.astype(BF16)], 0)
        rows16 = rows.astype(BF16)
        acc[which] += lax.dot_general(lhs, right_buf[i], NT, preferred_element_type=F32)
        col_acc[which] += lax.dot_general(rows16, ones, NT, preferred_element_type=F32)
        row_acc[which] += lax.dot_general(ones[:8], rows16, NT, preferred_element_type=F32)
        return carry

    lax.fori_loop(0, size, step, 0)
    if last:
        g = gain[...].astype(F32)

        def finish(l, carry):
            n = count[l].astype(F32)
            mean_out[pl.ds(l, 1), :] = row_acc[l, 0:1, :] / n
            sums = acc[l, ROW : ROW + 1, :] + acc[l, ROW + 1 : ROW + 2, :]
            co_out[l] = (acc[l, :ROW, :] - col_acc[l, :, 0:1] * (sums / n)) * (g / n)
            return carry

        lax.fori_loop(0, LANGS, finish, 0)


def gram(rights, left, meta, counts, gain):
    smem = pl.BlockSpec(memory_space=pltpu.SMEM)
    vmem = pl.BlockSpec(memory_space=pltpu.VMEM)
    far = pl.BlockSpec(memory_space=pl.ANY)
    state_shapes = [(LANGS, LROW, PANEL), (LANGS, 8, ROW), (LANGS, ROW, BLK)]
    state = []
    start = 0
    for n, size in enumerate(GROUPS):
        first, last = n == 0, n == len(GROUPS) - 1
        if last:
            out_shape = (
                jax.ShapeDtypeStruct((LANGS, ROW), F32),
                jax.ShapeDtypeStruct((LANGS, ROW, PANEL), F32),
            )
        else:
            out_shape = tuple(jax.ShapeDtypeStruct(s, F32) for s in state_shapes)
        held = len(state)
        state = pl.pallas_call(
            functools.partial(gram_kernel, first, size, last),
            out_shape=out_shape,
            in_specs=[smem] * 2 + [vmem] + [far] * (1 + size) + [vmem] * held,
            out_specs=tuple([vmem] * len(out_shape)),
            scratch_shapes=([pltpu.VMEM(s, F32) for s in state_shapes] if last else [])
            + [
                pltpu.VMEM((size, PANEL, SEQ), BF16),
                pltpu.VMEM((size, LROW, SEQ), BF16),
                pltpu.SemaphoreType.DMA((size,)),
                pltpu.SemaphoreType.DMA((size,)),
            ],
            input_output_aliases={} if last or first else {4 + size + k: k for k in range(3)},
            compiler_params=pltpu.CompilerParams(vmem_limit_bytes=40 << 20),
            name=f"gram{n}",
        )(meta[:, start : start + size], counts, gain, left, *rights[start : start + size], *state)
        start += size
    return state


def shards(inputs, queries, keys, values, out_weight, norm_gain, languages, lengths, pattern):
    dp = lax.axis_index("dp")
    mp = lax.axis_index("mp")
    my_y, my_z = dp // NZ, dp % NZ
    my_x, my_c = mp // 2, mp % 2
    language = languages[:, 0]
    onehot = language[:, None] == jnp.arange(LANGS)[None, :]
    counts = jnp.sum(onehot.astype(jnp.int32) * lengths[:, None], 0)

    mixed = attend(queries, keys, values, pattern[0])
    partial = lax.dot_general(
        out_weight, mixed, (((0,), (1,)), ((), ())), preferred_element_type=F32
    ).astype(BF16).reshape(NX, 2, PANEL, SEQ)
    other = lax.dynamic_index_in_dim(partial, 1 - my_c, 1, False)
    same = lax.dynamic_index_in_dim(partial, my_c, 1, False)
    pair = (same.astype(F32) + core_swap(other).astype(F32)).astype(BF16)

    def towards(r):
        return lax.dynamic_index_in_dim(pair, (my_x + r) % NX, 0, False)

    arrived = [x_step(towards(r), r) for r in (2, 1, 3)]
    output = towards(0).astype(F32) + sum(a.astype(F32) for a in arrived)
    hidden = inputs.T.astype(F32) + output
    block = hidden.astype(BF16)

    square = jnp.sum(hidden * hidden, 0, keepdims=True)
    square = square + core_swap(square)
    square = square + x_step(square, 1) + x_step(square, 2) + x_step(square, 3)
    scale = lax.rsqrt(square / D + epsilon)
    normed = (hidden * scale * norm_gain.astype(F32)[:, None]).astype(BF16)
    high = scale.astype(BF16)
    low = (scale - high.astype(F32)).astype(BF16)
    tail = jnp.concatenate([high, low, jnp.zeros((LROW - ROW - 2, SEQ), BF16)], 0)
    pieces = jnp.concatenate(
        [normed.reshape(4, ROW, SEQ), jnp.broadcast_to(tail[None], (4, LROW - ROW, SEQ))], 1
    )
    spread = []
    for t in range(4):
        piece = lax.dynamic_index_in_dim(pieces, (dp + t) % 4, 0, False)
        pairs = [
            ((4 * a + b) * 8 + p, (4 * p + (b + t) % 4) * 8 + a)
            for a in range(8) for b in range(4) for p in range(8)
        ]
        spread.append(lax.ppermute(piece, ("dp", "mp"), pairs))
    spread = jnp.stack(spread)
    ring = [spread] + [x_step(spread, r) for r in (1, 2, 3)]
    swapped = [core_swap(r) for r in ring]
    both = jnp.stack([jnp.stack([a, b]) for a, b in zip(ring, swapped)])
    order8 = jnp.arange(8)
    take_r = (my_x - order8 // 2) % NX
    take_c = (order8 % 2) ^ my_c
    left = jnp.stack(
        [lax.dynamic_slice(both, (take_r[k], take_c[k], 0, 0, 0), (1, 1, 4, LROW, SEQ))[0, 0] for k in range(8)]
    )

    order, rights = gather_all(block)
    back_y = jnp.array([o[0] for o in order], jnp.int32)
    back_z = jnp.array([o[1] for o in order], jnp.int32)
    seq = (my_y - back_y) % NY * NZ + (my_z - back_z) % NZ
    meta = jnp.stack([language[seq], lengths[seq], seq // 4, (dp - seq) % 4]).astype(jnp.int32)
    mean, co_moment = gram(rights, left, meta, counts, norm_gain[None, :])
    return (counts, mean, co_moment)


def solution(mesh):
    in_specs = (
        P("dp", "mp"),
        P("dp", "mp"),
        P("dp", "mp"),
        P("dp", "mp"),
        P("mp", None),
        P("mp"),
        P(),
        P(),
        P("dp", None, None),
    )
    out_specs = (P(), P(None, "dp"), P(None, "dp", "mp"))
    return jax.shard_map(shards, mesh=mesh, in_specs=in_specs, out_specs=out_specs, check_vma=False)
```

```python
import functools
import jax
import jax.numpy as jnp
from jax import lax
from jax.experimental import pallas as pl
from jax.experimental.pallas import tpu as pltpu
from jax.sharding import PartitionSpec as P

D = 4608
HD = 128
SEQ = 384
SEQS = 32
LANGS = 8
BLK = 128
NY, NZ, NX = 4, 8, 4
PANEL = 576
ROW = 144
LROW = 160

query_scale = 1.0 / 12.0
softcap = 50.0
epsilon = 1e-06


F32 = jnp.float32
BF16 = jnp.bfloat16
NT = (((1,), (1,)), ((), ()))


def front_kernel(place, q_ref, k_ref, v_ref, w_ref, pattern, mine, other, mixed):
    @pl.when(pl.program_id(0) == 0)
    def _():
        row = lax.broadcasted_iota(jnp.int32, (BLK, BLK), 0)
        col = lax.broadcasted_iota(jnp.int32, (BLK, BLK), 1)
        for h in range(4):
            g = h // 2
            for qb in range(3):
                query = q_ref[qb * BLK : (qb + 1) * BLK, h * HD : (h + 1) * HD]
                total = jnp.zeros((BLK, 1), F32)
                weights = []
                for kb in range(qb + 1):
                    key = k_ref[kb * BLK : (kb + 1) * BLK, g * HD : (g + 1) * HD]
                    score = lax.dot_general(query, key, NT, preferred_element_type=F32) * query_scale
                    expo = jnp.exp(softcap * jnp.tanh(score / softcap))
                    expo = expo * (pattern[0, qb, kb] == 1).astype(F32)
                    if kb == qb:
                        expo = jnp.where(col <= row, expo, 0.0)
                    total = total + jnp.sum(expo, 1, keepdims=True)
                    weights.append(expo)
                total = 1.0 / total
                out = jnp.zeros((BLK, HD), F32)
                for kb in range(qb + 1):
                    value = v_ref[kb * BLK : (kb + 1) * BLK, g * HD : (g + 1) * HD]
                    out = out + jnp.dot((weights[kb] * total).astype(BF16), value, preferred_element_type=F32)
                mixed[qb * BLK : (qb + 1) * BLK, h * HD : (h + 1) * HD] = out.astype(BF16)

    both = jnp.dot(mixed[...], w_ref[...], preferred_element_type=F32).astype(BF16).T

    @pl.when(place[1] == 0)
    def _():
        mine[0] = both[:PANEL]
        other[0] = both[PANEL:]

    @pl.when(place[1] == 1)
    def _():
        mine[0] = both[PANEL:]
        other[0] = both[:PANEL]


def front(place, queries, keys, values, out_weight, pattern):
    whole = lambda r, place: (0, 0)
    panels = jax.ShapeDtypeStruct((NX, PANEL, SEQ), BF16)
    out_spec = pl.BlockSpec((1, PANEL, SEQ), lambda r, place: (r, 0, 0))
    return pl.pallas_call(
        front_kernel,
        out_shape=(panels, panels),
        grid_spec=pltpu.PrefetchScalarGridSpec(
            num_scalar_prefetch=1,
            grid=(NX,),
            in_specs=[
                pl.BlockSpec((SEQ, 4 * HD), whole),
                pl.BlockSpec((SEQ, 2 * HD), whole),
                pl.BlockSpec((SEQ, 2 * HD), whole),
                pl.BlockSpec((4 * HD, 2 * PANEL), lambda r, place: (0, lax.rem(place[0] + r, NX))),
                pl.BlockSpec(memory_space=pltpu.SMEM),
            ],
            out_specs=(out_spec, out_spec),
            scratch_shapes=[pltpu.VMEM((SEQ, 4 * HD), BF16)],
        ),
        compiler_params=pltpu.CompilerParams(vmem_limit_bytes=20 << 20),
        name="front",
    )(place, *[pltpu.with_memory_space_constraint(a, pltpu.HBM) for a in (queries, keys, values, out_weight)], pattern)


def pair_kernel(mine, other, keep, one, two, three):
    for r, out in enumerate((keep, one, two, three)):
        out[...] = (mine[r].astype(F32) + other[r].astype(F32)).astype(BF16)


def hidden_kernel(x, keep, one, two, three, block, hidden, square):
    total = x[...].astype(F32) + keep[...].astype(F32) + one[...].astype(F32) + two[...].astype(F32) + three[...].astype(F32)
    hidden[...] = total
    block[...] = total.astype(BF16)
    square[...] = jnp.sum(total * total, 0, keepdims=True)


def norm_kernel(place, lengths, hidden, gain, keep, one, two, three, *rest):
    outs, tail = rest[:4], rest[4]
    square = keep[...] + one[...] + two[...] + three[...]
    scale = lax.rsqrt(square / D + epsilon)
    live = (lax.broadcasted_iota(jnp.int32, (1, SEQ), 1) < lengths[place[2]]).astype(F32)
    alive = scale * live
    high = alive.astype(BF16).astype(F32)
    tail[...] = jnp.zeros_like(tail)
    tail[0:1, :] = high
    tail[1:2, :] = alive - high
    mask = jnp.broadcast_to(live, (8, SEQ)).astype(BF16)
    for t, out in enumerate(outs):
        rows = pl.ds(pl.multiple_of(lax.rem(place[2] + t, 4) * ROW, 16), ROW)
        normed = hidden[rows, :] * scale * gain[rows, :]
        out[:ROW, :] = (normed * alive).astype(BF16)
        total = lax.dot_general(mask, normed.astype(BF16), NT, preferred_element_type=F32)[0:1]
        for n in range(3):
            part = total.astype(BF16).astype(F32)
            tail[2 + n : 3 + n, :ROW] = part
            total = total - part
        out[ROW:, :] = tail[...].astype(BF16)


def assemble_kernel(place, *refs):
    out = refs[8]
    for k in range(8):
        slot = 2 * lax.rem(place[0] + NX - k // 2, NX) + lax.rem(place[1] + k, 2)
        out[slot] = refs[k][...]


def small_call(kernel, out_shape, n_smem, *args, scratch=()):
    smem = pl.BlockSpec(memory_space=pltpu.SMEM)
    vmem = pl.BlockSpec(memory_space=pltpu.VMEM)
    return pl.pallas_call(
        kernel,
        out_shape=out_shape,
        in_specs=[smem] * n_smem + [vmem] * (len(args) - n_smem),
        out_specs=tuple([vmem] * len(out_shape)),
        scratch_shapes=list(scratch),
        compiler_params=pltpu.CompilerParams(vmem_limit_bytes=16 << 20),
    )(*args)


def dp_id(y, z):
    return (y % NY) * NZ + z % NZ


def mp_id(x, c):
    return (x % NX) * 2 + c


def dp_step(block, sy, sz):
    return lax.ppermute(
        block, "dp", [(dp_id(y, z), dp_id(y + sy, z + sz)) for y in range(NY) for z in range(NZ)]
    )


def x_step(block, s):
    return lax.ppermute(
        block, "mp", [(mp_id(x, c), mp_id(x + s, c)) for x in range(NX) for c in range(2)]
    )


def core_swap(block):
    return lax.ppermute(
        block, "mp", [(mp_id(x, c), mp_id(x, 1 - c)) for x in range(NX) for c in range(2)]
    )


TREE = [
    ((0, 1), 0, 1), ((0, -1), 0, -1), ((1, 0), 1, 0), ((-1, 0), -1, 0),
    ((0, 2), 0, 1), ((0, -2), 0, -1), ((1, 1), 1, 0), ((-1, -1), -1, 0),
    ((0, 3), 0, 1), ((0, -3), 0, -1), ((1, -1), 1, 0), ((-1, 1), -1, 0),
    ((1, 2), 0, 1), ((-1, -2), 0, -1), ((2, 1), 1, 0), ((-1, -3), -1, 0),
    ((-1, 2), 0, 1), ((1, -2), 0, -1), ((1, 3), 1, 0), ((2, -1), -1, 0),
    ((2, 2), 0, 1), ((-1, 4), 0, -1), ((1, -3), 1, 0), ((2, -3), -1, 0),
    ((1, 4), 0, 1), ((2, -2), 0, -1), ((2, 3), 1, 0), ((-1, 3), -1, 0),
    ((0, 4), 0, 1), ((2, 4), 0, -1), ((2, 0), -1, 0),
]
EARLY = 24


def canon(dy, dz):
    return (dy % NY, dz % NZ)


def gather_all(block):
    have = {(0, 0): block}
    order = [(0, 0)]
    for (dy, dz), sy, sz in TREE:
        key = canon(dy, dz)
        have[key] = dp_step(have[canon(dy - sy, dz - sz)], sy, sz)
        order.append(key)
    return order, [have[k] for k in order]


def gram_kernel(order, last, place, lang, *rest):
    size = len(order)
    if last:
        count, gain, left, acc_in, row_in = rest[:5]
        rights, rest = rest[5 : 5 + size], rest[5 + size :]
        mean_out, co_out, acc, row_acc, co_buf, out_sem = rest
        acc[...] = acc_in[...]
        row_acc[...] = row_in[...]
    else:
        left, rights, rest = rest[0], rest[1 : 1 + size], rest[1 + size :]
        acc, row_acc = rest
        acc[...] = jnp.zeros_like(acc)
        row_acc[...] = jnp.zeros_like(row_acc)
    mine = place[2]
    my_y, my_z = lax.div(mine, NZ), lax.rem(mine, NZ)
    for (dy, dz), right in zip(order, rights):
        s = lax.rem(my_y + (NY - dy), NY) * NZ + lax.rem(my_z + (NZ - dz), NZ)
        which = lang[s, 0]
        part = left[lax.div(s, 4), lax.rem(mine + SEQS - s, 4)]
        product = lax.dot_general(part, right[...], NT, preferred_element_type=F32)
        acc[which] += product
        row_acc[which] += part[ROW:].astype(F32)
    if last:
        g = gain[...].astype(F32)
        total = jnp.concatenate(
            [row_acc[l, 2:3, :ROW] + row_acc[l, 3:4, :ROW] + row_acc[l, 4:5, :ROW] for l in range(LANGS)], 0
        )
        eye = lax.broadcasted_iota(jnp.int32, (ROW, ROW), 0) == lax.broadcasted_iota(jnp.int32, (ROW, ROW), 1)
        column = lax.dot_general(
            eye.astype(F32), total, NT, precision=lax.Precision.HIGHEST, preferred_element_type=F32
        )
        for l in range(LANGS):
            n = count[l].astype(F32)
            mean_out[l : l + 1, :] = total[l : l + 1] / n
            sums = acc[l, ROW : ROW + 1, :] + acc[l, ROW + 1 : ROW + 2, :]
            co_buf[l] = (acc[l, :ROW, :] - column[:, l : l + 1] * (sums / n)) * (g / n)
            pltpu.make_async_copy(co_buf.at[l], co_out.at[l], out_sem.at[l]).start()
        for l in range(LANGS):
            pltpu.make_async_copy(co_buf.at[l], co_out.at[l], out_sem.at[l]).wait()


def gram(order, rights, left, place, language, counts, gain):
    smem = pl.BlockSpec(memory_space=pltpu.SMEM)
    vmem = pl.BlockSpec(memory_space=pltpu.VMEM)
    acc_shape, row_shape = (LANGS, LROW, PANEL), (LANGS, LROW - ROW, SEQ)
    params = pltpu.CompilerParams(vmem_limit_bytes=20 << 20)
    state = pl.pallas_call(
        functools.partial(gram_kernel, order[:EARLY], False),
        out_shape=(jax.ShapeDtypeStruct(acc_shape, F32), jax.ShapeDtypeStruct(row_shape, F32)),
        in_specs=[smem] * 2 + [vmem] * (1 + EARLY),
        out_specs=(vmem, vmem),
        compiler_params=params,
        name="gram0",
    )(place, language, left, *rights[:EARLY])
    return pl.pallas_call(
        functools.partial(gram_kernel, order[EARLY:], True),
        out_shape=(
            jax.ShapeDtypeStruct((LANGS, ROW), F32),
            jax.ShapeDtypeStruct((LANGS, ROW, PANEL), F32),
        ),
        in_specs=[smem] * 3 + [vmem] * (4 + len(order) - EARLY),
        out_specs=(vmem, pl.BlockSpec(memory_space=pltpu.HBM)),
        scratch_shapes=[
            pltpu.VMEM(acc_shape, F32),
            pltpu.VMEM(row_shape, F32),
            pltpu.VMEM((LANGS, ROW, PANEL), F32),
            pltpu.SemaphoreType.DMA((LANGS,)),
        ],
        compiler_params=params,
        name="gram1",
    )(place, language, counts, gain, left, *state, *rights[EARLY:])


def layer(inputs, queries, keys, values, out_weight, norm_gain, languages, lengths, pattern):
    dp = lax.axis_index("dp")
    mp = lax.axis_index("mp")
    place = jnp.stack([mp // 2, mp % 2, dp]).astype(jnp.int32)
    onehot = languages == jnp.arange(LANGS)[None, :]
    counts = jnp.sum(onehot.astype(jnp.int32) * lengths[:, None], 0)
    gain_column = norm_gain.astype(F32)[:, None]
    panel = jax.ShapeDtypeStruct((PANEL, SEQ), BF16)

    mine, other = front(place, queries, keys, values, out_weight, pattern)
    pair = small_call(pair_kernel, (panel,) * 4, 0, mine, core_swap(other))
    arrived = [x_step(pair[r], r) for r in (2, 1, 3)]
    block, hidden, square = small_call(
        hidden_kernel,
        (panel, jax.ShapeDtypeStruct((PANEL, SEQ), F32), jax.ShapeDtypeStruct((1, SEQ), F32)),
        0, inputs.T, pair[0], *arrived,
    )
    order, rights = gather_all(block)

    square = square + core_swap(square)
    squares = [square] + [x_step(square, r) for r in (1, 2, 3)]
    pieces = small_call(
        norm_kernel, (jax.ShapeDtypeStruct((LROW, SEQ), BF16),) * 4, 2, place, lengths, hidden, gain_column, *squares,
        scratch=[pltpu.VMEM((LROW - ROW, SEQ), F32)],
    )
    spread = []
    for t in range(4):
        pairs = [
            ((4 * a + b) * 8 + p, (4 * p + (b + t) % 4) * 8 + a)
            for a in range(8) for b in range(4) for p in range(8)
        ]
        spread.append(lax.ppermute(pieces[t], ("dp", "mp"), pairs))
    spread = jnp.stack(spread)
    ring = [spread] + [x_step(spread, r) for r in (1, 2, 3)]
    swapped = [core_swap(ring[r]) for r in range(4)]
    lefts = [half for r in range(4) for half in (ring[r], swapped[r])]
    (left,) = small_call(assemble_kernel, (jax.ShapeDtypeStruct((8, 4, LROW, SEQ), BF16),), 1, place, *lefts)
    mean, co_moment = gram(order, rights, left, place, languages, counts, norm_gain[None, :])
    return (counts, mean, co_moment)


def solution(mesh):
    in_specs = (
        P("dp", "mp"),
        P("dp", "mp"),
        P("dp", "mp"),
        P("dp", "mp"),
        P("mp", None),
        P("mp"),
        P(),
        P(),
        P("dp", None, None),
    )
    out_specs = (P(), P(None, "dp"), P(None, "dp", "mp"))
    return jax.shard_map(layer, mesh=mesh, in_specs=in_specs, out_specs=out_specs, check_vma=False)
```

```python
import functools
import jax
import jax.numpy as jnp
from jax import lax
from jax.experimental import pallas as pl
from jax.experimental.pallas import tpu as pltpu
from jax.sharding import PartitionSpec as P

D = 4608
HD = 128
SEQ = 384
SEQS = 32
LANGS = 8
BLK = 128
NY, NZ, NX = 4, 8, 4
PANEL = 576
ROW = 144
LROW = 160

query_scale = 1.0 / 12.0
softcap = 50.0
epsilon = 1e-06


F32 = jnp.float32
BF16 = jnp.bfloat16
NT = (((1,), (1,)), ((), ()))


def attention(q_ref, k_ref, v_ref, pattern, mixed):
    row = lax.broadcasted_iota(jnp.int32, (BLK, BLK), 0)
    col = lax.broadcasted_iota(jnp.int32, (BLK, BLK), 1)
    for h in range(4):
        g = h // 2
        for qb in range(3):
            query = q_ref[qb * BLK : (qb + 1) * BLK, h * HD : (h + 1) * HD]
            total = jnp.zeros((BLK, 1), F32)
            weights = []
            for kb in range(qb + 1):
                key = k_ref[kb * BLK : (kb + 1) * BLK, g * HD : (g + 1) * HD]
                score = lax.dot_general(query, key, NT, preferred_element_type=F32) * query_scale
                expo = jnp.exp(softcap * jnp.tanh(score / softcap))
                expo = expo * (pattern[0, qb, kb] == 1).astype(F32)
                if kb == qb:
                    expo = jnp.where(col <= row, expo, 0.0)
                total = total + jnp.sum(expo, 1, keepdims=True)
                weights.append(expo)
            total = 1.0 / total
            out = jnp.zeros((BLK, HD), F32)
            for kb in range(qb + 1):
                value = v_ref[kb * BLK : (kb + 1) * BLK, g * HD : (g + 1) * HD]
                out = out + jnp.dot((weights[kb] * total).astype(BF16), value, preferred_element_type=F32)
            mixed[qb * BLK : (qb + 1) * BLK, h * HD : (h + 1) * HD] = out.astype(BF16)


def project(place, w_ref, mixed, mine, other):
    both = jnp.dot(mixed[...], w_ref[...], preferred_element_type=F32).astype(BF16).T

    @pl.when(place[1] == 0)
    def _():
        mine[0] = both[:PANEL]
        other[0] = both[PANEL:]

    @pl.when(place[1] == 1)
    def _():
        mine[0] = both[PANEL:]
        other[0] = both[:PANEL]


def front0_kernel(place, w_ref, q_ref, k_ref, v_ref, pattern, mine, other, mixed):
    @pl.when(pl.program_id(0) == 0)
    def _():
        attention(q_ref, k_ref, v_ref, pattern, mixed)

    project(place, w_ref, mixed, mine, other)


def front1_kernel(place, w_ref, mixed, mine, other):
    project(place, w_ref, mixed, mine, other)


def front(kernel, ahead, mixed_out, place, out_weight, args, arg_specs):
    whole = lambda r, place: (0, 0)
    panels = jax.ShapeDtypeStruct((2, PANEL, SEQ), BF16)
    out_spec = pl.BlockSpec((1, PANEL, SEQ), lambda r, place: (r, 0, 0))
    mixed = jax.ShapeDtypeStruct((SEQ, 4 * HD), BF16)
    return pl.pallas_call(
        kernel,
        out_shape=(panels, panels) + ((mixed,) if mixed_out else ()),
        grid_spec=pltpu.PrefetchScalarGridSpec(
            num_scalar_prefetch=1,
            grid=(2,),
            in_specs=[
                pl.BlockSpec((4 * HD, 2 * PANEL), lambda r, place: (0, lax.rem(place[0] + ahead(r), NX))),
            ] + arg_specs,
            out_specs=(out_spec, out_spec) + ((pl.BlockSpec((SEQ, 4 * HD), whole),) if mixed_out else ()),
        ),
        compiler_params=pltpu.CompilerParams(vmem_limit_bytes=20 << 20),
    )(place, pltpu.with_memory_space_constraint(out_weight, pltpu.HBM), *args)


def pair_kernel(mine, other, one, two):
    for r, out in enumerate((one, two)):
        out[...] = (mine[r].astype(F32) + other[r].astype(F32)).astype(BF16)


def hidden_kernel(x, keep, one, two, three, block, hidden, square):
    total = x[...].astype(F32) + keep[...].astype(F32) + one[...].astype(F32) + two[...].astype(F32) + three[...].astype(F32)
    hidden[...] = total
    block[...] = total.astype(BF16)
    square[...] = jnp.sum(total * total, 0, keepdims=True)


def norm_kernel(place, lengths, hidden, gain, keep, one, two, three, *rest):
    outs, tail = rest[:4], rest[4]
    square = keep[...] + one[...] + two[...] + three[...]
    scale = lax.rsqrt(square / D + epsilon)
    live = (lax.broadcasted_iota(jnp.int32, (1, SEQ), 1) < lengths[place[2]]).astype(F32)
    alive = scale * live
    high = alive.astype(BF16).astype(F32)
    tail[...] = jnp.zeros_like(tail)
    tail[0:1, :] = high
    tail[1:2, :] = alive - high
    mask = jnp.broadcast_to(live, (8, SEQ)).astype(BF16)
    for t, out in enumerate(outs):
        rows = pl.ds(pl.multiple_of(lax.rem(place[2] + t, 4) * ROW, 16), ROW)
        normed = hidden[rows, :] * scale * gain[rows, :]
        out[:ROW, :] = (normed * alive).astype(BF16)
        total = lax.dot_general(mask, normed.astype(BF16), NT, preferred_element_type=F32)[0:1]
        for n in range(3):
            part = total.astype(BF16).astype(F32)
            tail[2 + n : 3 + n, :ROW] = part
            total = total - part
        out[ROW:, :] = tail[...].astype(BF16)


def assemble_kernel(place, *refs):
    out = refs[8]
    for k in range(8):
        slot = 2 * lax.rem(place[0] + NX - k // 2, NX) + lax.rem(place[1] + k, 2)
        out[slot] = refs[k][...]


def small_call(kernel, out_shape, n_smem, *args, scratch=()):
    smem = pl.BlockSpec(memory_space=pltpu.SMEM)
    vmem = pl.BlockSpec(memory_space=pltpu.VMEM)
    return pl.pallas_call(
        kernel,
        out_shape=out_shape,
        in_specs=[smem] * n_smem + [vmem] * (len(args) - n_smem),
        out_specs=tuple([vmem] * len(out_shape)),
        scratch_shapes=list(scratch),
        compiler_params=pltpu.CompilerParams(vmem_limit_bytes=16 << 20),
    )(*args)


def dp_id(y, z):
    return (y % NY) * NZ + z % NZ


def mp_id(x, c):
    return (x % NX) * 2 + c


def dp_step(block, sy, sz):
    return lax.ppermute(
        block, "dp", [(dp_id(y, z), dp_id(y + sy, z + sz)) for y in range(NY) for z in range(NZ)]
    )


def x_step(block, s):
    return lax.ppermute(
        block, "mp", [(mp_id(x, c), mp_id(x + s, c)) for x in range(NX) for c in range(2)]
    )


def core_swap(block):
    return lax.ppermute(
        block, "mp", [(mp_id(x, c), mp_id(x, 1 - c)) for x in range(NX) for c in range(2)]
    )


TREE = [
    ((0, 1), 0, 1), ((0, -1), 0, -1), ((1, 0), 1, 0), ((-1, 0), -1, 0),
    ((0, 2), 0, 1), ((0, -2), 0, -1), ((1, 1), 1, 0), ((-1, -1), -1, 0),
    ((0, 3), 0, 1), ((0, -3), 0, -1), ((1, -1), 1, 0), ((-1, 1), -1, 0),
    ((1, 2), 0, 1), ((-1, -2), 0, -1), ((2, 1), 1, 0), ((-1, -3), -1, 0),
    ((0, 4), 0, 1), ((1, -2), 0, -1), ((1, 3), 1, 0), ((2, -1), -1, 0),
    ((-1, 2), 0, 1), ((-1, 4), 0, -1), ((1, -3), 1, 0), ((2, -3), -1, 0),
    ((2, 2), 0, 1), ((2, -2), 0, -1), ((2, 3), 1, 0), ((-1, 3), -1, 0),
    ((2, 4), 0, -1), ((1, 4), 1, 0), ((2, 0), -1, 0),
]
SPLITS = (0, 24, 28, 32)


def canon(dy, dz):
    return (dy % NY, dz % NZ)


def gather_all(block):
    have = {(0, 0): block}
    order = [(0, 0)]
    for (dy, dz), sy, sz in TREE:
        key = canon(dy, dz)
        have[key] = dp_step(have[canon(dy - sy, dz - sz)], sy, sz)
        order.append(key)
    return order, [have[k] for k in order]


def gram_kernel(order, first, last, place, lang, *rest):
    size = len(order)
    if last:
        count, gain, rest = rest[0], rest[1], rest[2:]
    left, rights, rest = rest[0], rest[1 : 1 + size], rest[1 + size :]
    if not first:
        acc_in, row_in, rest = rest[0], rest[1], rest[2:]
    if last:
        mean_out, co_out, acc, row_acc, co_buf, out_sem = rest
    else:
        acc, row_acc = rest
    acc[...] = jnp.zeros_like(acc) if first else acc_in[...]
    row_acc[...] = jnp.zeros_like(row_acc) if first else row_in[...]
    mine = place[2]
    my_y, my_z = lax.div(mine, NZ), lax.rem(mine, NZ)
    for (dy, dz), right in zip(order, rights):
        s = lax.rem(my_y + (NY - dy), NY) * NZ + lax.rem(my_z + (NZ - dz), NZ)
        which = lang[s, 0]
        part = left[lax.div(s, 4), lax.rem(mine + SEQS - s, 4)]
        product = lax.dot_general(part, right[...], NT, preferred_element_type=F32)
        acc[which] += product
        row_acc[which] += part[ROW:].astype(F32)
    if last:
        g = gain[...].astype(F32)
        total = jnp.concatenate(
            [row_acc[l, 2:3, :ROW] + row_acc[l, 3:4, :ROW] + row_acc[l, 4:5, :ROW] for l in range(LANGS)], 0
        )
        eye = lax.broadcasted_iota(jnp.int32, (ROW, ROW), 0) == lax.broadcasted_iota(jnp.int32, (ROW, ROW), 1)
        column = lax.dot_general(
            eye.astype(F32), total, NT, precision=lax.Precision.HIGHEST, preferred_element_type=F32
        )
        for l in range(LANGS):
            n = count[l].astype(F32)
            mean_out[l : l + 1, :] = total[l : l + 1] / n
            sums = acc[l, ROW : ROW + 1, :] + acc[l, ROW + 1 : ROW + 2, :]
            co_buf[l] = (acc[l, :ROW, :] - column[:, l : l + 1] * (sums / n)) * (g / n)
            pltpu.make_async_copy(co_buf.at[l], co_out.at[l], out_sem.at[l]).start()
        for l in range(LANGS):
            pltpu.make_async_copy(co_buf.at[l], co_out.at[l], out_sem.at[l]).wait()


def gram(order, rights, left, place, language, counts, gain):
    smem = pl.BlockSpec(memory_space=pltpu.SMEM)
    vmem = pl.BlockSpec(memory_space=pltpu.VMEM)
    acc_shape, row_shape = (LANGS, LROW, PANEL), (LANGS, LROW - ROW, SEQ)
    params = pltpu.CompilerParams(vmem_limit_bytes=20 << 20)
    state = ()
    for n, (start, stop) in enumerate(zip(SPLITS, SPLITS[1:])):
        first, last = n == 0, stop == len(order)
        if last:
            out_shape = (
                jax.ShapeDtypeStruct((LANGS, ROW), F32),
                jax.ShapeDtypeStruct((LANGS, ROW, PANEL), F32),
            )
            scratch = [
                pltpu.VMEM(acc_shape, F32),
                pltpu.VMEM(row_shape, F32),
                pltpu.VMEM((LANGS, ROW, PANEL), F32),
                pltpu.SemaphoreType.DMA((LANGS,)),
            ]
        else:
            out_shape = (jax.ShapeDtypeStruct(acc_shape, F32), jax.ShapeDtypeStruct(row_shape, F32))
            scratch = []
        extra = (counts, gain) if last else ()
        extra_specs = [smem, vmem] if last else []
        state = pl.pallas_call(
            functools.partial(gram_kernel, order[start:stop], first, last),
            out_shape=out_shape,
            in_specs=[smem] * 2 + extra_specs + [vmem] * (1 + stop - start + len(state)),
            out_specs=(vmem, pl.BlockSpec(memory_space=pltpu.HBM) if last else vmem),
            scratch_shapes=scratch,
            compiler_params=params,
        )(place, language, *extra, left, *rights[start:stop], *state)
    return state


def layer(inputs, queries, keys, values, out_weight, norm_gain, languages, lengths, pattern):
    dp = lax.axis_index("dp")
    mp = lax.axis_index("mp")
    place = jnp.stack([mp // 2, mp % 2, dp]).astype(jnp.int32)
    onehot = languages == jnp.arange(LANGS)[None, :]
    counts = jnp.sum(onehot.astype(jnp.int32) * lengths[:, None], 0)
    gain_column = norm_gain.astype(F32)[:, None]
    panel = jax.ShapeDtypeStruct((PANEL, SEQ), BF16)

    whole = lambda r, place: (0, 0)
    near = lambda a: pltpu.with_memory_space_constraint(a, pltpu.HBM)
    mine0, other0, mixed = front(
        front0_kernel, lambda r: 2 - r, True, place, out_weight,
        [near(queries), near(keys), near(values), pattern],
        [pl.BlockSpec(a.shape, whole) for a in (queries, keys, values)] + [pl.BlockSpec(memory_space=pltpu.SMEM)],
    )
    mine1, other1 = front(
        front1_kernel, lambda r: 3 - 3 * r, False, place, out_weight,
        [mixed], [pl.BlockSpec((SEQ, 4 * HD), whole)],
    )
    two, one = small_call(pair_kernel, (panel,) * 2, 0, mine0, core_swap(other0))
    three, keep = small_call(pair_kernel, (panel,) * 2, 0, mine1, core_swap(other1))
    arrived = [x_step(p, r) for r, p in ((2, two), (1, one), (3, three))]
    block, hidden, square = small_call(
        hidden_kernel,
        (panel, jax.ShapeDtypeStruct((PANEL, SEQ), F32), jax.ShapeDtypeStruct((1, SEQ), F32)),
        0, inputs.T, keep, *arrived,
    )
    order, rights = gather_all(block)

    square = square + core_swap(square)
    squares = [square] + [x_step(square, r) for r in (1, 2, 3)]
    pieces = small_call(
        norm_kernel, (jax.ShapeDtypeStruct((LROW, SEQ), BF16),) * 4, 2, place, lengths, hidden, gain_column, *squares,
        scratch=[pltpu.VMEM((LROW - ROW, SEQ), F32)],
    )
    spread = []
    for t in range(4):
        pairs = [
            ((4 * a + b) * 8 + p, (4 * p + (b + t) % 4) * 8 + a)
            for a in range(8) for b in range(4) for p in range(8)
        ]
        spread.append(lax.ppermute(pieces[t], ("dp", "mp"), pairs))
    spread = jnp.stack(spread)
    ring = [spread] + [x_step(spread, r) for r in (1, 2, 3)]
    swapped = [core_swap(ring[r]) for r in range(4)]
    lefts = [half for r in range(4) for half in (ring[r], swapped[r])]
    (left,) = small_call(assemble_kernel, (jax.ShapeDtypeStruct((8, 4, LROW, SEQ), BF16),), 1, place, *lefts)
    mean, co_moment = gram(order, rights, left, place, languages, counts, norm_gain[None, :])
    return (counts, mean, co_moment)


def solution(mesh):
    in_specs = (
        P("dp", "mp"),
        P("dp", "mp"),
        P("dp", "mp"),
        P("dp", "mp"),
        P("mp", None),
        P("mp"),
        P(),
        P(),
        P("dp", None, None),
    )
    out_specs = (P(), P(None, "dp"), P(None, "dp", "mp"))
    return jax.shard_map(layer, mesh=mesh, in_specs=in_specs, out_specs=out_specs, check_vma=False)
```

```python
import functools
import jax
import jax.numpy as jnp
from jax import lax
from jax.experimental import pallas as pl
from jax.experimental.pallas import tpu as pltpu
from jax.sharding import PartitionSpec as P

D = 4608
HD = 128
SEQ = 384
SEQS = 32
LANGS = 8
BLK = 128
NY, NZ, NX = 4, 8, 4
PANEL = 576
ROW = 144
LROW = 160

query_scale = 1.0 / 12.0
softcap = 50.0
epsilon = 1e-06


F32 = jnp.float32
BF16 = jnp.bfloat16
NT = (((1,), (1,)), ((), ()))


def attention(q_ref, k_ref, v_ref, pattern, mixed):
    row = lax.broadcasted_iota(jnp.int32, (BLK, BLK), 0)
    col = lax.broadcasted_iota(jnp.int32, (BLK, BLK), 1)

    def head(h, carry):
        wide = pl.ds(pl.multiple_of(h * HD, HD), HD)
        narrow = pl.ds(pl.multiple_of(lax.div(h, 2) * HD, HD), HD)
        for qb in range(3):
            query = q_ref[qb * BLK : (qb + 1) * BLK, wide]
            total = jnp.zeros((BLK, 1), F32)
            weights = []
            for kb in range(qb + 1):
                key = k_ref[kb * BLK : (kb + 1) * BLK, narrow]
                score = lax.dot_general(query, key, NT, preferred_element_type=F32) * query_scale
                expo = jnp.exp(softcap * jnp.tanh(score / softcap))
                expo = expo * (pattern[0, qb, kb] == 1).astype(F32)
                if kb == qb:
                    expo = jnp.where(col <= row, expo, 0.0)
                total = total + jnp.sum(expo, 1, keepdims=True)
                weights.append(expo)
            total = 1.0 / total
            out = jnp.zeros((BLK, HD), F32)
            for kb in range(qb + 1):
                value = v_ref[kb * BLK : (kb + 1) * BLK, narrow]
                out = out + jnp.dot((weights[kb] * total).astype(BF16), value, preferred_element_type=F32)
            mixed[qb * BLK : (qb + 1) * BLK, wide] = out.astype(BF16)
        return carry

    lax.fori_loop(0, 4, head, 0)


def project(place, w_ref, mixed, mine, other):
    both = jnp.dot(mixed[...], w_ref[...], preferred_element_type=F32).astype(BF16).T

    @pl.when(place[1] == 0)
    def _():
        mine[0] = both[:PANEL]
        other[0] = both[PANEL:]

    @pl.when(place[1] == 1)
    def _():
        mine[0] = both[PANEL:]
        other[0] = both[:PANEL]


def front0_kernel(place, w_ref, q_ref, k_ref, v_ref, pattern, mine, other, mixed):
    @pl.when(pl.program_id(0) == 0)
    def _():
        attention(q_ref, k_ref, v_ref, pattern, mixed)

    project(place, w_ref, mixed, mine, other)


def front1_kernel(place, w_ref, mixed, mine, other):
    project(place, w_ref, mixed, mine, other)


def front(kernel, ahead, mixed_out, place, out_weight, args, arg_specs):
    whole = lambda r, place: (0, 0)
    panels = jax.ShapeDtypeStruct((2, PANEL, SEQ), BF16)
    out_spec = pl.BlockSpec((1, PANEL, SEQ), lambda r, place: (r, 0, 0))
    mixed = jax.ShapeDtypeStruct((SEQ, 4 * HD), BF16)
    return pl.pallas_call(
        kernel,
        out_shape=(panels, panels) + ((mixed,) if mixed_out else ()),
        grid_spec=pltpu.PrefetchScalarGridSpec(
            num_scalar_prefetch=1,
            grid=(2,),
            in_specs=[
                pl.BlockSpec((4 * HD, 2 * PANEL), lambda r, place: (0, lax.rem(place[0] + ahead(r), NX))),
            ] + arg_specs,
            out_specs=(out_spec, out_spec) + ((pl.BlockSpec((SEQ, 4 * HD), whole),) if mixed_out else ()),
        ),
        compiler_params=pltpu.CompilerParams(vmem_limit_bytes=20 << 20),
    )(place, pltpu.with_memory_space_constraint(out_weight, pltpu.HBM), *args)


def pair_kernel(mine, other, one, two):
    for r, out in enumerate((one, two)):
        out[...] = (mine[r].astype(F32) + other[r].astype(F32)).astype(BF16)


def hidden_kernel(x, keep, one, two, three, block, hidden, square):
    total = x[...].astype(F32) + keep[...].astype(F32) + one[...].astype(F32) + two[...].astype(F32) + three[...].astype(F32)
    hidden[...] = total
    block[...] = total.astype(BF16)
    square[...] = jnp.sum(total * total, 0, keepdims=True)


def norm_kernel(place, lengths, hidden, gain, square, *rest):
    outs, tail = rest[:4], rest[4]
    scale = lax.rsqrt(square[...] / D + epsilon)
    live = (lax.broadcasted_iota(jnp.int32, (1, SEQ), 1) < lengths[place[2]]).astype(F32)
    alive = scale * live
    high = alive.astype(BF16).astype(F32)
    tail[...] = jnp.zeros_like(tail)
    tail[0:1, :] = high
    tail[1:2, :] = alive - high
    mask = jnp.broadcast_to(live, (8, SEQ)).astype(BF16)
    for t, out in enumerate(outs):
        rows = pl.ds(pl.multiple_of(lax.rem(place[2] + t, 4) * ROW, 16), ROW)
        normed = hidden[rows, :] * scale * gain[rows, :]
        out[:ROW, :] = (normed * alive).astype(BF16)
        total = lax.dot_general(mask, normed.astype(BF16), NT, preferred_element_type=F32)[0:1]
        for n in range(3):
            part = total.astype(BF16).astype(F32)
            tail[2 + n : 3 + n, :ROW] = part
            total = total - part
        out[ROW:, :] = tail[...].astype(BF16)


def assemble_kernel(place, *refs):
    out = refs[8]
    for k in range(8):
        slot = 2 * lax.rem(place[0] + NX - k // 2, NX) + lax.rem(place[1] + k, 2)
        out[slot] = refs[k][...]


def small_call(kernel, out_shape, n_smem, *args, scratch=()):
    smem = pl.BlockSpec(memory_space=pltpu.SMEM)
    vmem = pl.BlockSpec(memory_space=pltpu.VMEM)
    return pl.pallas_call(
        kernel,
        out_shape=out_shape,
        in_specs=[smem] * n_smem + [vmem] * (len(args) - n_smem),
        out_specs=tuple([vmem] * len(out_shape)),
        scratch_shapes=list(scratch),
        compiler_params=pltpu.CompilerParams(vmem_limit_bytes=16 << 20),
    )(*args)


def dp_id(y, z):
    return (y % NY) * NZ + z % NZ


def mp_id(x, c):
    return (x % NX) * 2 + c


def dp_step(block, sy, sz):
    return lax.ppermute(
        block, "dp", [(dp_id(y, z), dp_id(y + sy, z + sz)) for y in range(NY) for z in range(NZ)]
    )


def x_step(block, s):
    return lax.ppermute(
        block, "mp", [(mp_id(x, c), mp_id(x + s, c)) for x in range(NX) for c in range(2)]
    )


def core_swap(block):
    return lax.ppermute(
        block, "mp", [(mp_id(x, c), mp_id(x, 1 - c)) for x in range(NX) for c in range(2)]
    )


TREE = [
    ([(0, 1)], 0, 1), ([(0, -1)], 0, -1), ([(1, 0)], 1, 0), ([(-1, 0)], -1, 0),
    ([(0, 2)], 0, 1), ([(0, -2)], 0, -1), ([(1, 1)], 1, 0), ([(-1, -1)], -1, 0),
    ([(0, 3)], 0, 1), ([(0, -3)], 0, -1), ([(1, -1)], 1, 0), ([(-1, 1)], -1, 0),
    ([(1, 2)], 0, 1), ([(-1, -2), (1, -2)], 0, -1), ([(2, 1)], 1, 0), ([(-1, -3)], -1, 0),
    ([(0, 4)], 0, 1), ([(1, 3)], 1, 0), ([(2, -1)], -1, 0),
    ([(-1, 2), (2, 2)], 0, 1), ([(-1, 4)], 0, -1), ([(1, -3)], 1, 0), ([(2, -3)], -1, 0),
    ([(2, -2), (2, 4)], 0, -1), ([(2, 3), (1, 4)], 1, 0), ([(-1, 3), (2, 0)], -1, 0),
]
SPLITS = (0, 22, 25, 27)


def canon(dy, dz):
    return (dy % NY, dz % NZ)


def gather_all(block):
    have = {(0, 0): block}
    order, arrays = [[(0, 0)]], [block]
    for offsets, sy, sz in TREE:
        sources = [have[canon(dy - sy, dz - sz)] for dy, dz in offsets]
        send = sources[0] if len(sources) == 1 else jnp.stack(sources)
        got = dp_step(send, sy, sz)
        if len(offsets) == 1:
            have[canon(*offsets[0])] = got
        order.append([canon(*o) for o in offsets])
        arrays.append(got)
    return order, arrays


def gram_kernel(order, first, last, place, lang, *rest):
    size = len(order)
    if last:
        count, gain, rest = rest[0], rest[1], rest[2:]
    left, rights, rest = rest[0], rest[1 : 1 + size], rest[1 + size :]
    if not first:
        acc_in, row_in, rest = rest[0], rest[1], rest[2:]
    if last:
        mean_out, co_out, acc, row_acc, co_buf, col_buf, out_sem = rest
    else:
        acc, row_acc = rest
    acc[...] = jnp.zeros_like(acc) if first else acc_in[...]
    row_acc[...] = jnp.zeros_like(row_acc) if first else row_in[...]
    mine = place[2]
    my_y, my_z = lax.div(mine, NZ), lax.rem(mine, NZ)
    pairs = [(o, ref, n) for group, ref in zip(order, rights) for n, o in enumerate(group)]
    for (dy, dz), ref, n in pairs:
        right = ref[...] if len(ref.shape) == 2 else ref[n]
        s = lax.rem(my_y + (NY - dy), NY) * NZ + lax.rem(my_z + (NZ - dz), NZ)
        which = lang[s, 0]
        part = left[lax.div(s, 4), lax.rem(mine + SEQS - s, 4)]
        product = lax.dot_general(part, right, NT, preferred_element_type=F32)
        acc[which] += product
        row_acc[which] += part[ROW:].astype(F32)
    if last:
        g = gain[...].astype(F32)
        total = jnp.concatenate(
            [row_acc[l, 2:3, :ROW] + row_acc[l, 3:4, :ROW] + row_acc[l, 4:5, :ROW] for l in range(LANGS)], 0
        )
        eye = lax.broadcasted_iota(jnp.int32, (ROW, ROW), 0) == lax.broadcasted_iota(jnp.int32, (ROW, ROW), 1)
        column = lax.dot_general(
            eye.astype(F32), total, NT, precision=lax.Precision.HIGHEST, preferred_element_type=F32
        )
        for l in range(LANGS):
            mean_out[l : l + 1, :] = total[l : l + 1] / count[l].astype(F32)
            col_buf[l] = column[:, l : l + 1]

        def finish(l, carry):
            n = count[l].astype(F32)
            sums = acc[l, ROW : ROW + 1, :] + acc[l, ROW + 1 : ROW + 2, :]
            co_buf[l] = (acc[l, :ROW, :] - col_buf[l] * (sums / n)) * (g / n)
            pltpu.make_async_copy(co_buf.at[l], co_out.at[l], out_sem.at[l]).start()
            return carry

        lax.fori_loop(0, LANGS, finish, 0)
        for l in range(LANGS):
            pltpu.make_async_copy(co_buf.at[l], co_out.at[l], out_sem.at[l]).wait()


def gram(order, rights, left, place, language, counts, gain):
    smem = pl.BlockSpec(memory_space=pltpu.SMEM)
    vmem = pl.BlockSpec(memory_space=pltpu.VMEM)
    acc_shape, row_shape = (LANGS, LROW, PANEL), (LANGS, LROW - ROW, SEQ)
    params = pltpu.CompilerParams(vmem_limit_bytes=20 << 20)
    state = ()
    for n, (start, stop) in enumerate(zip(SPLITS, SPLITS[1:])):
        first, last = n == 0, stop == len(order)
        if last:
            out_shape = (
                jax.ShapeDtypeStruct((LANGS, ROW), F32),
                jax.ShapeDtypeStruct((LANGS, ROW, PANEL), F32),
            )
            scratch = [
                pltpu.VMEM(acc_shape, F32),
                pltpu.VMEM(row_shape, F32),
                pltpu.VMEM((LANGS, ROW, PANEL), F32),
                pltpu.VMEM((LANGS, ROW, 1), F32),
                pltpu.SemaphoreType.DMA((LANGS,)),
            ]
        else:
            out_shape = (jax.ShapeDtypeStruct(acc_shape, F32), jax.ShapeDtypeStruct(row_shape, F32))
            scratch = []
        extra = (counts, gain) if last else ()
        extra_specs = [smem, vmem] if last else []
        state = pl.pallas_call(
            functools.partial(gram_kernel, order[start:stop], first, last),
            out_shape=out_shape,
            in_specs=[smem] * 2 + extra_specs + [vmem] * (1 + stop - start + len(state)),
            out_specs=(vmem, pl.BlockSpec(memory_space=pltpu.HBM) if last else vmem),
            scratch_shapes=scratch,
            compiler_params=params,
        )(place, language, *extra, left, *rights[start:stop], *state)
    return state


def layer(inputs, queries, keys, values, out_weight, norm_gain, languages, lengths, pattern):
    dp = lax.axis_index("dp")
    mp = lax.axis_index("mp")
    place = jnp.stack([mp // 2, mp % 2, dp]).astype(jnp.int32)
    onehot = languages == jnp.arange(LANGS)[None, :]
    counts = jnp.sum(onehot.astype(jnp.int32) * lengths[:, None], 0)
    gain_column = norm_gain.astype(F32)[:, None]
    panel = jax.ShapeDtypeStruct((PANEL, SEQ), BF16)

    whole = lambda r, place: (0, 0)
    near = lambda a: pltpu.with_memory_space_constraint(a, pltpu.HBM)
    mine0, other0, mixed = front(
        front0_kernel, lambda r: 2 - r, True, place, out_weight,
        [near(queries), near(keys), near(values), pattern],
        [pl.BlockSpec(a.shape, whole) for a in (queries, keys, values)] + [pl.BlockSpec(memory_space=pltpu.SMEM)],
    )
    mine1, other1 = front(
        front1_kernel, lambda r: 3 - 3 * r, False, place, out_weight,
        [mixed], [pl.BlockSpec((SEQ, 4 * HD), whole)],
    )
    two, one = small_call(pair_kernel, (panel,) * 2, 0, mine0, core_swap(other0))
    three, keep = small_call(pair_kernel, (panel,) * 2, 0, mine1, core_swap(other1))
    arrived = [x_step(p, r) for r, p in ((2, two), (1, one), (3, three))]
    block, hidden, square = small_call(
        hidden_kernel,
        (panel, jax.ShapeDtypeStruct((PANEL, SEQ), F32), jax.ShapeDtypeStruct((1, SEQ), F32)),
        0, inputs.T, keep, *arrived,
    )
    order, rights = gather_all(block)

    square = square + core_swap(square)
    for bit in (1, 2):
        square = square + lax.ppermute(
            square, "mp", [(mp_id(x, c), mp_id(x ^ bit, c)) for x in range(NX) for c in range(2)]
        )
    pieces = small_call(
        norm_kernel, (jax.ShapeDtypeStruct((LROW, SEQ), BF16),) * 4, 2, place, lengths, hidden, gain_column, square,
        scratch=[pltpu.VMEM((LROW - ROW, SEQ), F32)],
    )
    spread = []
    for t in range(4):
        pairs = [
            ((4 * a + b) * 8 + p, (4 * p + (b + t) % 4) * 8 + a)
            for a in range(8) for b in range(4) for p in range(8)
        ]
        spread.append(lax.ppermute(pieces[t], ("dp", "mp"), pairs))
    spread = jnp.stack(spread)
    ring = [spread] + [x_step(spread, r) for r in (1, 2, 3)]
    swapped = [core_swap(ring[r]) for r in range(4)]
    lefts = [half for r in range(4) for half in (ring[r], swapped[r])]
    (left,) = small_call(assemble_kernel, (jax.ShapeDtypeStruct((8, 4, LROW, SEQ), BF16),), 1, place, *lefts)
    mean, co_moment = gram(order, rights, left, place, languages, counts, norm_gain[None, :])
    return (counts, mean, co_moment)


def solution(mesh):
    in_specs = (
        P("dp", "mp"),
        P("dp", "mp"),
        P("dp", "mp"),
        P("dp", "mp"),
        P("mp", None),
        P("mp"),
        P(),
        P(),
        P("dp", None, None),
    )
    out_specs = (P(), P(None, "dp"), P(None, "dp", "mp"))
    return jax.shard_map(layer, mesh=mesh, in_specs=in_specs, out_specs=out_specs, check_vma=False)
```

```python
import functools
import jax
import jax.numpy as jnp
from jax import lax
from jax.experimental import pallas as pl
from jax.experimental.pallas import tpu as pltpu
from jax.sharding import PartitionSpec as P

D = 4608
HD = 128
SEQ = 384
SEQS = 32
LANGS = 8
BLK = 128
NY, NZ, NX = 4, 8, 4
PANEL = 576
ROW = 144
LROW = 160

query_scale = 1.0 / 12.0
softcap = 50.0
epsilon = 1e-06


F32 = jnp.float32
BF16 = jnp.bfloat16
NT = (((1,), (1,)), ((), ()))


def attention(q_ref, k_ref, v_ref, pattern, mixed):
    row = lax.broadcasted_iota(jnp.int32, (BLK, BLK), 0)
    col = lax.broadcasted_iota(jnp.int32, (BLK, BLK), 1)
    for h in range(4):
        g = h // 2
        for qb in range(3):
            query = q_ref[qb * BLK : (qb + 1) * BLK, h * HD : (h + 1) * HD]
            total = jnp.zeros((BLK, 1), F32)
            weights = []
            for kb in range(qb + 1):
                key = k_ref[kb * BLK : (kb + 1) * BLK, g * HD : (g + 1) * HD]
                score = lax.dot_general(query, key, NT, preferred_element_type=F32) * query_scale
                expo = jnp.exp(softcap * jnp.tanh(score / softcap))
                expo = expo * (pattern[0, qb, kb] == 1).astype(F32)
                if kb == qb:
                    expo = jnp.where(col <= row, expo, 0.0)
                total = total + jnp.sum(expo, 1, keepdims=True)
                weights.append(expo)
            total = 1.0 / total
            out = jnp.zeros((BLK, HD), F32)
            for kb in range(qb + 1):
                value = v_ref[kb * BLK : (kb + 1) * BLK, g * HD : (g + 1) * HD]
                out = out + jnp.dot((weights[kb] * total).astype(BF16), value, preferred_element_type=F32)
            mixed[qb * BLK : (qb + 1) * BLK, h * HD : (h + 1) * HD] = out.astype(BF16)


def project(place, w_ref, mixed, mine, other):
    both = jnp.dot(mixed[...], w_ref[...], preferred_element_type=F32).astype(BF16).T

    @pl.when(place[1] == 0)
    def _():
        mine[0] = both[:PANEL]
        other[0] = both[PANEL:]

    @pl.when(place[1] == 1)
    def _():
        mine[0] = both[PANEL:]
        other[0] = both[:PANEL]


def front0_kernel(place, w_ref, q_ref, k_ref, v_ref, pattern, mine, other, mixed):
    @pl.when(pl.program_id(0) == 0)
    def _():
        attention(q_ref, k_ref, v_ref, pattern, mixed)

    project(place, w_ref, mixed, mine, other)


def front1_kernel(place, w_ref, mixed, mine, other):
    project(place, w_ref, mixed, mine, other)


def front(kernel, ahead, mixed_out, place, out_weight, args, arg_specs):
    whole = lambda r, place: (0, 0)
    panels = jax.ShapeDtypeStruct((2, PANEL, SEQ), BF16)
    out_spec = pl.BlockSpec((1, PANEL, SEQ), lambda r, place: (r, 0, 0))
    mixed = jax.ShapeDtypeStruct((SEQ, 4 * HD), BF16)
    return pl.pallas_call(
        kernel,
        out_shape=(panels, panels) + ((mixed,) if mixed_out else ()),
        grid_spec=pltpu.PrefetchScalarGridSpec(
            num_scalar_prefetch=1,
            grid=(2,),
            in_specs=[
                pl.BlockSpec((4 * HD, 2 * PANEL), lambda r, place: (0, lax.rem(place[0] + ahead(r), NX))),
            ] + arg_specs,
            out_specs=(out_spec, out_spec) + ((pl.BlockSpec((SEQ, 4 * HD), whole),) if mixed_out else ()),
        ),
        compiler_params=pltpu.CompilerParams(vmem_limit_bytes=20 << 20),
    )(place, pltpu.with_memory_space_constraint(out_weight, pltpu.HBM), *args)


def pair_kernel(mine, other, one, two):
    for r, out in enumerate((one, two)):
        out[...] = (mine[r].astype(F32) + other[r].astype(F32)).astype(BF16)


def hidden_kernel(x, keep, one, two, three, block, hidden, square):
    total = x[...].astype(F32) + keep[...].astype(F32) + one[...].astype(F32) + two[...].astype(F32) + three[...].astype(F32)
    hidden[...] = total
    block[...] = total.astype(BF16)
    square[...] = jnp.sum(total * total, 0, keepdims=True)


def norm_kernel(place, lengths, hidden, gain, keep, one, two, three, *rest):
    outs, tail = rest[:4], rest[4]
    square = keep[...] + one[...] + two[...] + three[...]
    scale = lax.rsqrt(square / D + epsilon)
    live = (lax.broadcasted_iota(jnp.int32, (1, SEQ), 1) < lengths[place[2]]).astype(F32)
    alive = scale * live
    high = alive.astype(BF16).astype(F32)
    tail[...] = jnp.zeros_like(tail)
    tail[0:1, :] = high
    tail[1:2, :] = alive - high
    mask = jnp.broadcast_to(live, (8, SEQ)).astype(BF16)
    for t, out in enumerate(outs):
        rows = pl.ds(pl.multiple_of(lax.rem(place[2] + t, 4) * ROW, 16), ROW)
        normed = hidden[rows, :] * scale * gain[rows, :]
        out[:ROW, :] = (normed * alive).astype(BF16)
        total = lax.dot_general(mask, normed.astype(BF16), NT, preferred_element_type=F32)[0:1]
        for n in range(3):
            part = total.astype(BF16).astype(F32)
            tail[2 + n : 3 + n, :ROW] = part
            total = total - part
        out[ROW:, :] = tail[...].astype(BF16)


def assemble_kernel(place, *refs):
    out = refs[8]
    for k in range(8):
        slot = 2 * lax.rem(place[0] + NX - k // 2, NX) + lax.rem(place[1] + k, 2)
        out[slot] = refs[k][...]


def small_call(kernel, out_shape, n_smem, *args, scratch=()):
    smem = pl.BlockSpec(memory_space=pltpu.SMEM)
    vmem = pl.BlockSpec(memory_space=pltpu.VMEM)
    return pl.pallas_call(
        kernel,
        out_shape=out_shape,
        in_specs=[smem] * n_smem + [vmem] * (len(args) - n_smem),
        out_specs=tuple([vmem] * len(out_shape)),
        scratch_shapes=list(scratch),
        compiler_params=pltpu.CompilerParams(vmem_limit_bytes=16 << 20),
    )(*args)


def dp_id(y, z):
    return (y % NY) * NZ + z % NZ


def mp_id(x, c):
    return (x % NX) * 2 + c


def dp_step(block, sy, sz):
    return lax.ppermute(
        block, "dp", [(dp_id(y, z), dp_id(y + sy, z + sz)) for y in range(NY) for z in range(NZ)]
    )


def x_step(block, s):
    return lax.ppermute(
        block, "mp", [(mp_id(x, c), mp_id(x + s, c)) for x in range(NX) for c in range(2)]
    )


def core_swap(block):
    return lax.ppermute(
        block, "mp", [(mp_id(x, c), mp_id(x, 1 - c)) for x in range(NX) for c in range(2)]
    )


TREE = [
    ((0, 1), 0, 1), ((0, -1), 0, -1), ((1, 0), 1, 0), ((-1, 0), -1, 0),
    ((0, 2), 0, 1), ((0, -2), 0, -1), ((1, 1), 1, 0), ((-1, -1), -1, 0),
    ((0, 3), 0, 1), ((0, -3), 0, -1), ((1, -1), 1, 0), ((-1, 1), -1, 0),
    ((1, 2), 0, 1), ((-1, -2), 0, -1), ((2, 1), 1, 0), ((-1, -3), -1, 0),
    ((0, 4), 0, 1), ((1, -2), 0, -1), ((1, 3), 1, 0), ((2, -1), -1, 0),
    ((-1, 2), 0, 1), ((-1, 4), 0, -1), ((1, -3), 1, 0), ((2, -3), -1, 0),
    ((2, 2), 0, 1), ((2, -2), 0, -1), ((2, 3), 1, 0), ((-1, 3), -1, 0),
    ((2, 4), 0, -1), ((1, 4), 1, 0), ((2, 0), -1, 0),
]
SPLITS = (0, 24, 28, 32)


def canon(dy, dz):
    return (dy % NY, dz % NZ)


def gather_all(block):
    have = {(0, 0): block}
    order = [(0, 0)]
    for (dy, dz), sy, sz in TREE:
        key = canon(dy, dz)
        have[key] = dp_step(have[canon(dy - sy, dz - sz)], sy, sz)
        order.append(key)
    return order, [have[k] for k in order]


def gram_kernel(order, first, last, place, lang, *rest):
    size = len(order)
    if last:
        count, gain, rest = rest[0], rest[1], rest[2:]
    left, rights, rest = rest[0], rest[1 : 1 + size], rest[1 + size :]
    if not first:
        acc_in, row_in, rest = rest[0], rest[1], rest[2:]
    if last:
        mean_out, co_out, acc, row_acc, co_buf, col_buf, out_sem = rest
    else:
        acc, row_acc = rest
    acc[...] = jnp.zeros_like(acc) if first else acc_in[...]
    row_acc[...] = jnp.zeros_like(row_acc) if first else row_in[...]
    mine = place[2]
    my_y, my_z = lax.div(mine, NZ), lax.rem(mine, NZ)
    for (dy, dz), right in zip(order, rights):
        s = lax.rem(my_y + (NY - dy), NY) * NZ + lax.rem(my_z + (NZ - dz), NZ)
        which = lang[s, 0]
        part = left[lax.div(s, 4), lax.rem(mine + SEQS - s, 4)]
        product = lax.dot_general(part, right[...], NT, preferred_element_type=F32)
        acc[which] += product
        row_acc[which] += part[ROW:].astype(F32)
    if last:
        g = gain[...].astype(F32)
        total = jnp.concatenate(
            [row_acc[l, 2:3, :ROW] + row_acc[l, 3:4, :ROW] + row_acc[l, 4:5, :ROW] for l in range(LANGS)], 0
        )
        eye = lax.broadcasted_iota(jnp.int32, (ROW, ROW), 0) == lax.broadcasted_iota(jnp.int32, (ROW, ROW), 1)
        column = lax.dot_general(
            eye.astype(F32), total, NT, precision=lax.Precision.HIGHEST, preferred_element_type=F32
        )
        for l in range(LANGS):
            mean_out[l : l + 1, :] = total[l : l + 1] / count[l].astype(F32)
            col_buf[l] = column[:, l : l + 1]

        def finish(l, carry):
            n = count[l].astype(F32)
            sums = acc[l, ROW : ROW + 1, :] + acc[l, ROW + 1 : ROW + 2, :]
            co_buf[l] = (acc[l, :ROW, :] - col_buf[l] * (sums / n)) * (g / n)
            pltpu.make_async_copy(co_buf.at[l], co_out.at[l], out_sem.at[l]).start()
            return carry

        lax.fori_loop(0, LANGS, finish, 0)
        for l in range(LANGS):
            pltpu.make_async_copy(co_buf.at[l], co_out.at[l], out_sem.at[l]).wait()


def gram(order, rights, left, place, language, counts, gain):
    smem = pl.BlockSpec(memory_space=pltpu.SMEM)
    vmem = pl.BlockSpec(memory_space=pltpu.VMEM)
    acc_shape, row_shape = (LANGS, LROW, PANEL), (LANGS, LROW - ROW, SEQ)
    params = pltpu.CompilerParams(vmem_limit_bytes=20 << 20)
    state = ()
    for n, (start, stop) in enumerate(zip(SPLITS, SPLITS[1:])):
        first, last = n == 0, stop == len(order)
        if last:
            out_shape = (
                jax.ShapeDtypeStruct((LANGS, ROW), F32),
                jax.ShapeDtypeStruct((LANGS, ROW, PANEL), F32),
            )
            scratch = [
                pltpu.VMEM(acc_shape, F32),
                pltpu.VMEM(row_shape, F32),
                pltpu.VMEM((LANGS, ROW, PANEL), F32),
                pltpu.VMEM((LANGS, ROW, 1), F32),
                pltpu.SemaphoreType.DMA((LANGS,)),
            ]
        else:
            out_shape = (jax.ShapeDtypeStruct(acc_shape, F32), jax.ShapeDtypeStruct(row_shape, F32))
            scratch = []
        extra = (counts, gain) if last else ()
        extra_specs = [smem, vmem] if last else []
        state = pl.pallas_call(
            functools.partial(gram_kernel, order[start:stop], first, last),
            out_shape=out_shape,
            in_specs=[smem] * 2 + extra_specs + [vmem] * (1 + stop - start + len(state)),
            out_specs=(vmem, pl.BlockSpec(memory_space=pltpu.HBM) if last else vmem),
            scratch_shapes=scratch,
            compiler_params=params,
        )(place, language, *extra, left, *rights[start:stop], *state)
    return state


def layer(inputs, queries, keys, values, out_weight, norm_gain, languages, lengths, pattern):
    dp = lax.axis_index("dp")
    mp = lax.axis_index("mp")
    place = jnp.stack([mp // 2, mp % 2, dp]).astype(jnp.int32)
    onehot = languages == jnp.arange(LANGS)[None, :]
    counts = jnp.sum(onehot.astype(jnp.int32) * lengths[:, None], 0)
    gain_column = norm_gain.astype(F32)[:, None]
    panel = jax.ShapeDtypeStruct((PANEL, SEQ), BF16)

    whole = lambda r, place: (0, 0)
    near = lambda a: pltpu.with_memory_space_constraint(a, pltpu.HBM)
    mine0, other0, mixed = front(
        front0_kernel, lambda r: 2 - r, True, place, out_weight,
        [near(queries), near(keys), near(values), pattern],
        [pl.BlockSpec(a.shape, whole) for a in (queries, keys, values)] + [pl.BlockSpec(memory_space=pltpu.SMEM)],
    )
    mine1, other1 = front(
        front1_kernel, lambda r: 3 - 3 * r, False, place, out_weight,
        [mixed], [pl.BlockSpec((SEQ, 4 * HD), whole)],
    )
    two, one = small_call(pair_kernel, (panel,) * 2, 0, mine0, core_swap(other0))
    three, keep = small_call(pair_kernel, (panel,) * 2, 0, mine1, core_swap(other1))
    arrived = [x_step(p, r) for r, p in ((2, two), (1, one), (3, three))]
    block, hidden, square = small_call(
        hidden_kernel,
        (panel, jax.ShapeDtypeStruct((PANEL, SEQ), F32), jax.ShapeDtypeStruct((1, SEQ), F32)),
        0, inputs.T, keep, *arrived,
    )
    order, rights = gather_all(block)

    square = square + core_swap(square)
    squares = [square] + [x_step(square, r) for r in (1, 2, 3)]
    pieces = small_call(
        norm_kernel, (jax.ShapeDtypeStruct((LROW, SEQ), BF16),) * 4, 2, place, lengths, hidden, gain_column, *squares,
        scratch=[pltpu.VMEM((LROW - ROW, SEQ), F32)],
    )
    spread = []
    for t in range(4):
        pairs = [
            ((4 * a + b) * 8 + p, (4 * p + (b + t) % 4) * 8 + a)
            for a in range(8) for b in range(4) for p in range(8)
        ]
        spread.append(lax.ppermute(pieces[t], ("dp", "mp"), pairs))
    spread = jnp.stack(spread)
    ring = [spread] + [x_step(spread, r) for r in (1, 2, 3)]
    swapped = [core_swap(ring[r]) for r in range(4)]
    lefts = [half for r in range(4) for half in (ring[r], swapped[r])]
    (left,) = small_call(assemble_kernel, (jax.ShapeDtypeStruct((8, 4, LROW, SEQ), BF16),), 1, place, *lefts)
    mean, co_moment = gram(order, rights, left, place, languages, counts, norm_gain[None, :])
    return (counts, mean, co_moment)


def solution(mesh):
    in_specs = (
        P("dp", "mp"),
        P("dp", "mp"),
        P("dp", "mp"),
        P("dp", "mp"),
        P("mp", None),
        P("mp"),
        P(),
        P(),
        P("dp", None, None),
    )
    out_specs = (P(), P(None, "dp"), P(None, "dp", "mp"))
    return jax.shard_map(layer, mesh=mesh, in_specs=in_specs, out_specs=out_specs, check_vma=False)
```
